32 devices in a mesh: row: 8 (over y, x, core), col: 4 (over z).
Axes of the slice: x: 2, y: 2, z: 4, core: 2. Of those that a mesh axis runs over, the one named last changes fastest.
Arguments:
- tokens: bfloat16 [65536, 1024], P('row', 'col'), may hold values from -6 to 6
- up_weight: bfloat16 [1024, 4096], P('row', 'col'), may hold values from -0.1875 to 0.1875
- hidden_grad: bfloat16 [65536, 4096], P('row', 'col'), may hold values from -6 to 6
Outputs:
- hidden: bfloat16 [65536, 4096], P('row', 'col')
- input_grad: bfloat16 [65536, 1024], P('row', 'col')
The draws below stay inside these ranges and needn't reach their ends.
All inputs are finite; a program needn't handle non-finite values.
Results may differ from the reference program's by a relative error of at most 0.017.
Values may be sent and summed in bfloat16 or wider, within the bound.
No kernel may reach another device: no remote copies, remote signals or barrier semaphores. Data moves between devices by JAX's collectives and lax.ppermute only.
A program may use at most 128 MiB of HBM per device.

```python
import jax
import jax.numpy as jnp
from jax import lax

D = 1024
FF = 4096
TOKENS = 65536
HID_BLOCK = 1024


def levels(own_key, dims, shards, least, high):
    def one(position, blocks):
        steps = jax.random.uniform(jax.random.fold_in(jax.random.fold_in(own_key, 6), position), (blocks,), jnp.float32, least / len(shards), high / len(shards))
        return jnp.repeat(jnp.exp(steps), dims[position] // blocks).reshape((-1,) + (1,) * (len(dims) - position - 1))

    factor_of = one(*shards[0])
    for cut in shards[1:]:
        factor_of = factor_of * one(*cut)
    return factor_of


def noise(own_key, shape, scale, reach, pieces=(), kind=jnp.bfloat16):
    entries = scale * jax.random.normal(own_key, shape, jnp.float32)
    if pieces:
        entries = entries * levels(own_key, shape, pieces, -0.22, 0.18)
    return jnp.clip(entries, -reach, reach).astype(kind)


def setup_inputs(seed: int = 0) -> dict:
    seeds = jax.random.split(jax.random.key(seed), 4)
    tokens = noise(seeds[0], (TOKENS, D), 1.0, 6.0, ((0, 8), (1, 4)))
    up_weight = noise(seeds[1], (D, FF), D ** -0.5, 0.1875, ((0, 8), (1, 4)))
    hidden_grad = noise(seeds[2], (TOKENS, FF), 1.0, 6.0, ((0, 8), (1, 4)))
    return {"tokens": tokens, "up_weight": up_weight, "hidden_grad": hidden_grad}


gelu_c = 0.7978845608028654
gelu_a = 0.044715


def gelu_value(v):
    inner = gelu_c * (v + gelu_a * v * v * v)
    return 0.5 * v * (1.0 + jnp.tanh(inner))


def gelu_slope(v):
    inner = gelu_c * (v + gelu_a * v * v * v)
    tval = jnp.tanh(inner)
    return 0.5 * (1.0 + tval) + 0.5 * v * (1.0 - tval * tval) * gelu_c * (1.0 + 3.0 * gelu_a * v * v)


def reference(tokens, up_weight, hidden_grad):
    def one_block(running_total, block_index):
        begin_col = (block_index * HID_BLOCK).astype(jnp.int32)
        weights_block = lax.dynamic_slice_in_dim(up_weight, begin_col, HID_BLOCK, 1)
        preact = jnp.dot(tokens, weights_block, preferred_element_type=jnp.float32)
        hidden_block = gelu_value(preact).astype(jnp.bfloat16)
        grads_block = lax.dynamic_slice_in_dim(hidden_grad, begin_col, HID_BLOCK, 1)
        pre_grad = (grads_block.astype(jnp.float32) * gelu_slope(preact)).astype(jnp.bfloat16)
        term = lax.dot_general(pre_grad, weights_block, (((1,), (1,)), ((), ())), preferred_element_type=jnp.float32).astype(jnp.bfloat16)
        term = lax.optimization_barrier(term)
        return running_total + term.astype(jnp.float32), hidden_block

    blocks = jnp.arange(FF // HID_BLOCK, dtype=jnp.int32)
    start_total = jnp.zeros((TOKENS, D), jnp.float32)
    input_grad, hidden_blocks = lax.scan(one_block, start_total, blocks)
    hidden = jnp.transpose(hidden_blocks, (1, 0, 2)).reshape(TOKENS, FF)
    return hidden, input_grad.astype(jnp.bfloat16)
```

```python
import jax
import jax.numpy as jnp
from jax import lax
from jax.experimental import pallas as pl
from jax.experimental.pallas import tpu as pltpu
from jax.sharding import PartitionSpec as P


gelu_c = 0.7978845608028654
gelu_a = 0.044715


shares = (1, 1, 2, 2, 2, 2, 2, 2, 1, 1)


def gelu_value(v):
    inner = gelu_c * (v + gelu_a * v * v * v)
    return 0.5 * v * (1.0 + jnp.tanh(inner))


def gelu_slope(v):
    inner = gelu_c * (v + gelu_a * v * v * v)
    tval = jnp.tanh(inner)
    return 0.5 * (1.0 + tval) + 0.5 * v * (1.0 - tval * tval) * gelu_c * (
        1.0 + 3.0 * gelu_a * v * v
    )


def plain_device(tokens, up_weight, hidden_grad):
    column_panel = lax.all_gather(up_weight, "row", axis=0, tiled=True)
    token_rows = lax.all_gather(tokens, "col", axis=1, tiled=True)
    preact = jnp.dot(token_rows, column_panel, preferred_element_type=jnp.float32)
    hidden = gelu_value(preact).astype(jnp.bfloat16)
    pre_grad = (hidden_grad.astype(jnp.float32) * gelu_slope(preact)).astype(jnp.bfloat16)
    summed = lax.psum_scatter(
        lax.dot_general(
            column_panel, pre_grad, (((1,), (1,)), ((), ())), preferred_element_type=jnp.float32
        ).astype(jnp.bfloat16),
        "col",
        scatter_dimension=0,
        tiled=True,
    ).astype(jnp.float32)
    input_grad = jnp.transpose(summed).astype(jnp.bfloat16)
    return (hidden, input_grad)


def chunk_kernel(place, near_ref, inner_ref, outer_ref, w_ref, wt_ref, grad_ref, *rest):
    hidden_ref, far_out, near_out = rest[-3:]
    half = near_ref.shape[1]
    near_at = pl.multiple_of(place[0] * half, half)
    far_at = pl.multiple_of((1 - place[0]) * half, half)
    far = jnp.where(place[1] == 1, inner_ref[...], outer_ref[...])
    v = jnp.dot(near_ref[...], w_ref[pl.ds(near_at, half), :], preferred_element_type=jnp.float32)
    v = v + jnp.dot(far, w_ref[pl.ds(far_at, half), :], preferred_element_type=jnp.float32)
    square = v * v
    tval = jnp.tanh(gelu_c * (v + gelu_a * square * v))
    gate = 0.5 * (1.0 + tval)
    hidden_ref[...] = (v * gate).astype(hidden_ref.dtype)
    slope = gate + 0.5 * v * (1.0 - tval * tval) * gelu_c * (1.0 + 3.0 * gelu_a * square)
    pre_grad = (grad_ref[...].astype(jnp.float32) * slope).astype(jnp.bfloat16)
    far_out[...] = jnp.dot(
        pre_grad, wt_ref[:, pl.ds(far_at, half)], preferred_element_type=jnp.float32
    ).astype(far_out.dtype)
    near_out[...] = jnp.dot(
        pre_grad, wt_ref[:, pl.ds(near_at, half)], preferred_element_type=jnp.float32
    ).astype(near_out.dtype)


def chunk_call(place, near, inner, outer, w, wt, grad, hidden, row_at):
    size, half = near.shape
    rows, width = grad.shape
    tile = 256 if size % 256 == 0 else size
    first = row_at // tile
    features = w.shape[0]
    args = [place, near, inner, outer, w, wt, grad]
    in_specs = [
        pl.BlockSpec((tile, half), lambda i, p: (i, 0)),
        pl.BlockSpec((tile, half), lambda i, p: (i * p[1], 0)),
        pl.BlockSpec((tile, half), lambda i, p: (i * (1 - p[1]), 0)),
        pl.BlockSpec((features, width), lambda i, p: (0, 0)),
        pl.BlockSpec((width, features), lambda i, p: (0, 0)),
        pl.BlockSpec((tile, width), lambda i, p: (first + i, 0)),
    ]
    aliases = {}
    if hidden is not None:
        aliases = {len(args): 0}
        args.append(hidden)
        in_specs.append(pl.BlockSpec(memory_space=pl.ANY))
    return pl.pallas_call(
        chunk_kernel,
        grid_spec=pltpu.PrefetchScalarGridSpec(
            num_scalar_prefetch=1,
            grid=(size // tile,),
            in_specs=in_specs,
            out_specs=[
                pl.BlockSpec((tile, width), lambda i, p: (first + i, 0)),
                pl.BlockSpec((tile, half), lambda i, p: (i, 0)),
                pl.BlockSpec((tile, half), lambda i, p: (i, 0)),
            ],
        ),
        out_shape=[
            jax.ShapeDtypeStruct((rows, width), jnp.bfloat16),
            jax.ShapeDtypeStruct((size, half), jnp.bfloat16),
            jax.ShapeDtypeStruct((size, half), jnp.bfloat16),
        ],
        input_output_aliases=aliases,
        compiler_params=pltpu.CompilerParams(vmem_limit_bytes=40 * 1024 * 1024),
        cost_estimate=pl.CostEstimate(
            flops=4 * size * features * width,
            bytes_accessed=size * (8 * half + 4 * width) + 4 * features * width,
            transcendentals=size * width,
        ),
    )(*args)


def panel_kernel(me_ref, block_ref, w_ref, wt_ref):
    w_ref[...] = block_ref[...]
    wt_ref[...] = jnp.transpose(block_ref[...])


def gather_panel(up_weight, n_row):
    me = lax.axis_index("row").astype(jnp.int32)
    block = up_weight
    bits = n_row.bit_length() - 1
    for step in range(bits):
        bit = n_row >> (step + 1)
        other = lax.ppermute(block, "row", [(i, i ^ bit) for i in range(n_row)])
        block = jnp.concatenate([block, other], axis=0)
    depth, width = up_weight.shape

    def place_of(j, p):
        apart = j ^ p[0]
        at = 0
        for step in range(bits):
            at = at + ((apart >> (bits - 1 - step)) & 1) * (1 << step)
        return at

    return pl.pallas_call(
        panel_kernel,
        grid_spec=pltpu.PrefetchScalarGridSpec(
            num_scalar_prefetch=1,
            grid=(n_row,),
            in_specs=[pl.BlockSpec((depth, width), lambda j, p: (place_of(j, p), 0))],
            out_specs=[
                pl.BlockSpec((depth, width), lambda j, p: (j, 0)),
                pl.BlockSpec((width, depth), lambda j, p: (0, j)),
            ],
        ),
        out_shape=[
            jax.ShapeDtypeStruct((n_row * depth, width), up_weight.dtype),
            jax.ShapeDtypeStruct((width, n_row * depth), up_weight.dtype),
        ],
        cost_estimate=pl.CostEstimate(
            flops=0, bytes_accessed=6 * n_row * depth * width, transcendentals=0
        ),
    )(me.reshape(1), block)


def line_device(n_row, tokens, up_weight, hidden_grad):
    col = lax.axis_index("col")
    odd = (col % 2) == 1
    pair = [(0, 1), (1, 0), (2, 3), (3, 2)]
    middle = [(1, 2), (2, 1)]
    outward = [(1, 0), (2, 3)]
    inward = [(0, 1), (3, 2)]

    def send(x, pairs):
        return lax.ppermute(x, "col", pairs)

    rows, block = tokens.shape
    unit = rows // sum(shares)
    place = jnp.stack([col // 2, ((col == 1) | (col == 2)).astype(jnp.int32)]).astype(jnp.int32)

    w, wt = gather_panel(up_weight, n_row)

    hidden = None
    input_grad = jnp.zeros((rows, block), jnp.bfloat16)
    at = 0
    for share in shares:
        size = share * unit
        own = lax.slice_in_dim(tokens, at, at + size, axis=0)
        partner = send(own, pair)
        near = jnp.where(
            odd, jnp.concatenate([partner, own], axis=1), jnp.concatenate([own, partner], axis=1)
        )
        inner = send(near, middle)
        outer = send(inner, outward)
        hidden, far_part, near_part = chunk_call(
            place, near, inner, outer, w, wt, hidden_grad, hidden, at
        )
        from_end = send(far_part, inward)
        across = (far_part.astype(jnp.float32) + from_end.astype(jnp.float32)).astype(jnp.bfloat16)
        from_far = send(across, middle)
        mine = near_part.astype(jnp.float32) + from_far.astype(jnp.float32)
        low, high = mine[:, :block], mine[:, block:]
        for_partner = jnp.where(odd, low, high).astype(jnp.bfloat16)
        from_partner = send(for_partner, pair)
        total = (jnp.where(odd, high, low) + from_partner.astype(jnp.float32)).astype(jnp.bfloat16)
        input_grad = lax.dynamic_update_slice(input_grad, total, (at, 0))
        at += size
    return (hidden, input_grad)


def fits_line(mesh, tokens, up_weight):
    n_row, n_col = mesh.shape["row"], mesh.shape["col"]
    rows, block = tokens.shape[0] // n_row, tokens.shape[1] // n_col
    return (
        n_col == 4
        and n_row & (n_row - 1) == 0
        and rows % (16 * sum(shares)) == 0
        and block % 128 == 0
        and up_weight.shape[1] % (128 * n_col) == 0
    )


def solution(mesh):
    specs = (P("row", "col"), P("row", "col"), P("row", "col"))

    def line_body(*blocks):
        return line_device(mesh.shape["row"], *blocks)

    def mapped(body):
        return jax.shard_map(body, mesh=mesh, in_specs=specs, out_specs=specs[:2], check_vma=False)

    ordered = mapped(line_body)

    def whole(tokens, up_weight, hidden_grad):
        if fits_line(mesh, tokens, up_weight):
            return ordered(tokens, up_weight, hidden_grad)
        return mapped(plain_device)(tokens, up_weight, hidden_grad)

    return whole
```

```python
import functools

import jax
import jax.numpy as jnp
from jax import lax
from jax.experimental import pallas as pl
from jax.experimental.pallas import tpu as pltpu
from jax.sharding import PartitionSpec as P


gelu_c = 0.7978845608028654
gelu_a = 0.044715


shares = (1, 2, 3, 4, 4, 4, 4, 4, 3, 2, 1)

groups = (1, 2, 2, 2, 2, 2)


def gelu_value(v):
    inner = gelu_c * (v + gelu_a * v * v * v)
    return 0.5 * v * (1.0 + jnp.tanh(inner))


def gelu_slope(v):
    inner = gelu_c * (v + gelu_a * v * v * v)
    tval = jnp.tanh(inner)
    return 0.5 * (1.0 + tval) + 0.5 * v * (1.0 - tval * tval) * gelu_c * (
        1.0 + 3.0 * gelu_a * v * v
    )


def plain_device(tokens, up_weight, hidden_grad):
    column_panel = lax.all_gather(up_weight, "row", axis=0, tiled=True)
    token_rows = lax.all_gather(tokens, "col", axis=1, tiled=True)
    preact = jnp.dot(token_rows, column_panel, preferred_element_type=jnp.float32)
    hidden = gelu_value(preact).astype(jnp.bfloat16)
    pre_grad = (hidden_grad.astype(jnp.float32) * gelu_slope(preact)).astype(jnp.bfloat16)
    summed = lax.psum_scatter(
        lax.dot_general(
            column_panel, pre_grad, (((1,), (1,)), ((), ())), preferred_element_type=jnp.float32
        ).astype(jnp.bfloat16),
        "col",
        scatter_dimension=0,
        tiled=True,
    ).astype(jnp.float32)
    input_grad = jnp.transpose(summed).astype(jnp.bfloat16)
    return (hidden, input_grad)


def fill_panel(me, depth, kept_ref, got_ref, w_ref):
    half = kept_ref.shape[0] // depth
    bits = half.bit_length()
    for source, base in ((kept_ref, 0), (got_ref, half)):

        @pl.loop(0, half)
        def _(j):
            index = me
            for step in range(bits):
                index = index ^ ((((j + base) >> step) & 1) << (bits - 1 - step))
            here = pl.ds(pl.multiple_of(index * depth, depth), depth)
            w_ref[here, :] = source[pl.ds(pl.multiple_of(j * depth, depth), depth), :]


def chunk_kernel(
    depth, place, own, out_in, mid_in, cross, spread, kept_ref, got_ref, grad_ref, *rest
):
    hidden_ref, send_ref, keep_ref, w_ref = rest[-4:]

    @pl.when(pl.program_id(0) == 0)
    def _():
        fill_panel(place[5], depth, kept_ref, got_ref, w_ref)

    block = own.shape[1]
    at = [pl.ds(pl.multiple_of(place[i] * block, block), block) for i in range(4)]
    middle = place[4] == 1
    partner = jnp.where(middle, out_in[...], mid_in[...])
    far = jnp.where(middle, cross[...], spread[...])
    v = jnp.dot(own[...], w_ref[at[0], :], preferred_element_type=jnp.float32)
    v = v + jnp.dot(partner, w_ref[at[1], :], preferred_element_type=jnp.float32)
    v = v + jnp.dot(far[:, :block], w_ref[at[2], :], preferred_element_type=jnp.float32)
    v = v + jnp.dot(far[:, block:], w_ref[at[3], :], preferred_element_type=jnp.float32)
    square = v * v
    tval = jnp.tanh(gelu_c * (v + gelu_a * square * v))
    gate = 0.5 * (1.0 + tval)
    hidden_ref[...] = (v * gate).astype(hidden_ref.dtype)
    slope = gate + 0.5 * v * (1.0 - tval * tval) * gelu_c * (1.0 + 3.0 * gelu_a * square)
    pre_grad = (grad_ref[...].astype(jnp.float32) * slope).astype(jnp.bfloat16)

    def term(i):
        got = lax.dot_general(
            pre_grad, w_ref[at[i], :], (((1,), (1,)), ((), ())), preferred_element_type=jnp.float32
        )
        return got.astype(jnp.bfloat16)

    send_ref[:, :block] = term(2)
    send_ref[:, block : 2 * block] = term(3)
    send_ref[:, 2 * block :] = term(1)
    keep_ref[...] = term(0)


def chunk_call(place, tokens, out_in, mid_in, cross, spread, panel, grad, hidden, at, start):
    size, block = cross.shape[0], tokens.shape[1]
    rows, width = grad.shape
    tile = 256 if size % 256 == 0 else size
    first, in_group = at // tile, (at - start) // tile
    depth, kept, got = panel
    half = kept.shape[0]
    features = 2 * half
    args = [place, tokens, out_in, mid_in, cross, spread, kept, got, grad]
    here = lambda i, p: (i, 0)
    at_middle = lambda i, p: (i * p[4], 0)
    at_outer = lambda i, p: (i * (1 - p[4]), 0)
    all_rows = lambda i, p: (i + first, 0)
    in_specs = [
        pl.BlockSpec((tile, block), all_rows),
        pl.BlockSpec((tile, block), lambda i, p: ((i + in_group) * p[4], 0)),
        pl.BlockSpec((tile, block), lambda i, p: ((i + in_group) * (1 - p[4]), 0)),
        pl.BlockSpec((tile, 2 * block), at_middle),
        pl.BlockSpec((tile, 2 * block), at_outer),
        pl.BlockSpec((half, width), lambda i, p: (0, 0)),
        pl.BlockSpec((half, width), lambda i, p: (0, 0)),
        pl.BlockSpec((tile, width), all_rows),
    ]
    aliases = {}
    if hidden is not None:
        aliases = {len(args): 0}
        args.append(hidden)
        in_specs.append(pl.BlockSpec(memory_space=pl.ANY))
    return pl.pallas_call(
        functools.partial(chunk_kernel, depth),
        grid_spec=pltpu.PrefetchScalarGridSpec(
            num_scalar_prefetch=1,
            grid=(size // tile,),
            in_specs=in_specs,
            out_specs=[
                pl.BlockSpec((tile, width), all_rows),
                pl.BlockSpec((tile, 3 * block), here),
                pl.BlockSpec((tile, block), here),
            ],
            scratch_shapes=[pltpu.VMEM((features, width), jnp.bfloat16)],
        ),
        out_shape=[
            jax.ShapeDtypeStruct((rows, width), jnp.bfloat16),
            jax.ShapeDtypeStruct((size, 3 * block), jnp.bfloat16),
            jax.ShapeDtypeStruct((size, block), jnp.bfloat16),
        ],
        input_output_aliases=aliases,
        compiler_params=pltpu.CompilerParams(vmem_limit_bytes=40 * 1024 * 1024),
        cost_estimate=pl.CostEstimate(
            flops=4 * size * features * width,
            bytes_accessed=size * (16 * block + 4 * width) + 2 * features * width,
            transcendentals=size * width,
        ),
    )(*args)


def gather_panel(up_weight, n_row):
    bits = n_row.bit_length() - 1
    kept = up_weight
    for step in range(bits):
        bit = n_row >> (step + 1)
        got = lax.ppermute(kept, "row", [(i, i ^ bit) for i in range(n_row)])
        if step < bits - 1:
            kept = jnp.concatenate([kept, got], axis=0)
    return up_weight.shape[0], kept, got


def line_device(n_row, tokens, up_weight, hidden_grad):
    col = lax.axis_index("col").astype(jnp.int32)
    inward = [(0, 1), (3, 2)]
    outward = [(1, 0), (2, 3)]
    across = [(1, 2), (2, 1)]

    def send(x, pairs):
        return lax.ppermute(x, "col", pairs)

    rows, block = tokens.shape
    unit = rows // sum(shares)
    half = col // 2
    is_middle = ((col == 1) | (col == 2)).astype(jnp.int32)
    place = [col, col ^ 1, 2 - half, 3 * (1 - half), is_middle]
    place = jnp.stack(place + [lax.axis_index("row").astype(jnp.int32)])

    panel = gather_panel(up_weight, n_row)

    grouped = []
    at = 0
    for index, count in enumerate(groups):
        first = sum(groups[:index])
        start, at = at, at + unit * sum(shares[first : first + count])
        own = lax.slice_in_dim(tokens, start, at, axis=0)
        pair = (send(own, inward), send(own, outward))
        grouped += [(start,) + pair] * count

    hidden = None
    input_grad = jnp.zeros((rows, block), jnp.bfloat16)
    at = 0
    for index, share in enumerate(shares):
        size = share * unit
        start, out_in, mid_in = grouped[index]
        own = lax.slice_in_dim(tokens, at, at + size, axis=0)
        theirs = lax.slice_in_dim(out_in, at - start, at - start + size, axis=0)
        both = jnp.concatenate([own, theirs], axis=1)
        cross = send(both, across)
        spread = send(cross, outward)
        hidden, terms, keep = chunk_call(
            place, tokens, out_in, mid_in, cross, spread, panel, hidden_grad, hidden, at, start
        )
        got = send(terms, inward)
        far = terms[:, : 2 * block].astype(jnp.float32) + got[:, : 2 * block].astype(jnp.float32)
        far = far.astype(jnp.bfloat16)
        back = send(far, across)
        theirs = terms[:, 2 * block :].astype(jnp.float32) + back[:, block:].astype(jnp.float32)
        theirs = theirs.astype(jnp.bfloat16)
        last = send(theirs, outward)
        total = keep.astype(jnp.float32) + back[:, :block].astype(jnp.float32)
        total = total + got[:, 2 * block :].astype(jnp.float32) + last.astype(jnp.float32)
        input_grad = lax.dynamic_update_slice(input_grad, total.astype(jnp.bfloat16), (at, 0))
        at += size
    return (hidden, input_grad)


def fits_line(mesh, tokens, up_weight):
    n_row, n_col = mesh.shape["row"], mesh.shape["col"]
    rows, block = tokens.shape[0] // n_row, tokens.shape[1] // n_col
    return (
        n_col == 4
        and n_row > 1
        and n_row & (n_row - 1) == 0
        and rows % (16 * sum(shares)) == 0
        and block % 128 == 0
        and up_weight.shape[1] % (128 * n_col) == 0
    )


def solution(mesh):
    specs = (P("row", "col"), P("row", "col"), P("row", "col"))

    def line_body(*blocks):
        return line_device(mesh.shape["row"], *blocks)

    def mapped(body):
        return jax.shard_map(body, mesh=mesh, in_specs=specs, out_specs=specs[:2], check_vma=False)

    ordered = mapped(line_body)

    def whole(tokens, up_weight, hidden_grad):
        if fits_line(mesh, tokens, up_weight):
            return ordered(tokens, up_weight, hidden_grad)
        return mapped(plain_device)(tokens, up_weight, hidden_grad)

    return whole
```

```python
import functools

import jax
import jax.numpy as jnp
from jax import lax
from jax.experimental import pallas as pl
from jax.experimental.pallas import tpu as pltpu
from jax.sharding import PartitionSpec as P


gelu_c = 0.7978845608028654
gelu_a = 0.044715


shares = (1, 3, 5, 6, 6, 5, 4, 2)

groups = (1, 1, 1, 1, 1, 1, 2)

ahead, late_parts, late_backs = 2, 5, 3


def gelu_value(v):
    inner = gelu_c * (v + gelu_a * v * v * v)
    return 0.5 * v * (1.0 + jnp.tanh(inner))


def gelu_slope(v):
    inner = gelu_c * (v + gelu_a * v * v * v)
    tval = jnp.tanh(inner)
    return 0.5 * (1.0 + tval) + 0.5 * v * (1.0 - tval * tval) * gelu_c * (
        1.0 + 3.0 * gelu_a * v * v
    )


def plain_device(tokens, up_weight, hidden_grad):
    column_panel = lax.all_gather(up_weight, "row", axis=0, tiled=True)
    token_rows = lax.all_gather(tokens, "col", axis=1, tiled=True)
    preact = jnp.dot(token_rows, column_panel, preferred_element_type=jnp.float32)
    hidden = gelu_value(preact).astype(jnp.bfloat16)
    pre_grad = (hidden_grad.astype(jnp.float32) * gelu_slope(preact)).astype(jnp.bfloat16)
    summed = lax.psum_scatter(
        lax.dot_general(
            column_panel, pre_grad, (((1,), (1,)), ((), ())), preferred_element_type=jnp.float32
        ).astype(jnp.bfloat16),
        "col",
        scatter_dimension=0,
        tiled=True,
    ).astype(jnp.float32)
    input_grad = jnp.transpose(summed).astype(jnp.bfloat16)
    return (hidden, input_grad)


def fill_panel(me, depth, kept_ref, got_ref, w_ref):
    half = kept_ref.shape[0] // depth
    bits = half.bit_length()
    for source, base in ((kept_ref, 0), (got_ref, half)):

        @pl.loop(0, half)
        def _(j):
            index = me
            for step in range(bits):
                index = index ^ ((((j + base) >> step) & 1) << (bits - 1 - step))
            here = pl.ds(pl.multiple_of(index * depth, depth), depth)
            w_ref[here, :] = source[pl.ds(pl.multiple_of(j * depth, depth), depth), :]


def chunk_kernel(
    depth, terms, place, own, out_in, mid_in, cross_a, cross_b, spread_a, spread_b, kept_ref, got_ref, grad_ref, *rest
):
    hidden_ref, *term_refs, w_ref = rest[-2 - terms :]

    @pl.when(pl.program_id(0) == 0)
    def _():
        fill_panel(place[5], depth, kept_ref, got_ref, w_ref)

    block = own.shape[1]
    at = [pl.ds(pl.multiple_of(place[i] * block, block), block) for i in range(4)]
    middle = place[4] == 1
    partner = jnp.where(middle, out_in[...], mid_in[...])
    far_middle = jnp.where(middle, cross_a[...], spread_a[...])
    far_outer = jnp.where(middle, cross_b[...], spread_b[...])
    v = jnp.dot(own[...], w_ref[at[0], :], preferred_element_type=jnp.float32)
    v = v + jnp.dot(partner, w_ref[at[1], :], preferred_element_type=jnp.float32)
    v = v + jnp.dot(far_middle, w_ref[at[2], :], preferred_element_type=jnp.float32)
    v = v + jnp.dot(far_outer, w_ref[at[3], :], preferred_element_type=jnp.float32)
    square = v * v
    tval = jnp.tanh(gelu_c * (v + gelu_a * square * v))
    gate = 0.5 * (1.0 + tval)
    hidden_ref[...] = (v * gate).astype(hidden_ref.dtype)
    slope = gate + 0.5 * v * (1.0 - tval * tval) * gelu_c * (1.0 + 3.0 * gelu_a * square)
    pre_grad = (grad_ref[...].astype(jnp.float32) * slope).astype(jnp.bfloat16)

    def term(i):
        got = lax.dot_general(
            pre_grad, w_ref[at[i], :], (((1,), (1,)), ((), ())), preferred_element_type=jnp.float32
        )
        return got.astype(jnp.bfloat16)

    where = [(0, 0), (0, 1), (0, 2), (1, 0)] if terms == 2 else [(0, 0), (0, 1), (1, 0), (2, 0)]
    for (ref, slot), i in zip(where, (2, 3, 1, 0)):
        term_refs[ref][:, slot * block : (slot + 1) * block] = term(i)


def chunk_call(place, size, tokens, out_in, mid_in, cross, spread, panel, grad, hidden, at, start, widths):
    block = tokens.shape[1]
    rows, width = grad.shape
    tile = 256 if size % 256 == 0 else size
    first = at // tile
    depth, kept, got = panel
    half = kept.shape[0]
    features = 2 * half
    pieces = [*cross, *spread]
    args = [place, tokens, out_in, mid_in, *[x for x, _, _ in pieces], kept, got, grad]
    here = lambda i, p: (i, 0)


    def piece(column, row, wanted):
        tiles = row // tile
        return pl.BlockSpec((tile, block), lambda i, p: ((i + tiles) * wanted(p), column))

    on_middle, on_outer = lambda p: p[4], lambda p: 1 - p[4]
    all_rows = lambda i, p: (i + first, 0)
    in_specs = [
        pl.BlockSpec((tile, block), all_rows),
        piece(0, at - start, on_middle),
        piece(0, at - start, on_outer),
        *[piece(column, row, on_middle) for _, column, row in cross],
        *[piece(column, row, on_outer) for _, column, row in spread],
        pl.BlockSpec((half, width), lambda i, p: (0, 0)),
        pl.BlockSpec((half, width), lambda i, p: (0, 0)),
        pl.BlockSpec((tile, width), all_rows),
    ]
    aliases = {}
    if hidden is not None:
        aliases = {len(args): 0}
        args.append(hidden)
        in_specs.append(pl.BlockSpec(memory_space=pl.ANY))
    return pl.pallas_call(
        functools.partial(chunk_kernel, depth, len(widths)),
        grid_spec=pltpu.PrefetchScalarGridSpec(
            num_scalar_prefetch=1,
            grid=(size // tile,),
            in_specs=in_specs,
            out_specs=[
                pl.BlockSpec((tile, width), all_rows),
                *[pl.BlockSpec((tile, n * block), here) for n in widths],
            ],
            scratch_shapes=[pltpu.VMEM((features, width), jnp.bfloat16)],
        ),
        out_shape=[
            jax.ShapeDtypeStruct((rows, width), jnp.bfloat16),
            *[jax.ShapeDtypeStruct((size, n * block), jnp.bfloat16) for n in widths],
        ],
        input_output_aliases=aliases,
        compiler_params=pltpu.CompilerParams(vmem_limit_bytes=40 * 1024 * 1024),
        cost_estimate=pl.CostEstimate(
            flops=4 * size * features * width,
            bytes_accessed=size * (16 * block + 4 * width) + 2 * features * width,
            transcendentals=size * width,
        ),
    )(*args)


def gather_panel(up_weight, n_row):
    bits = n_row.bit_length() - 1
    kept = up_weight
    for step in range(bits):
        bit = n_row >> (step + 1)
        got = lax.ppermute(kept, "row", [(i, i ^ bit) for i in range(n_row)])
        if step < bits - 1:
            kept = jnp.concatenate([kept, got], axis=0)
    return up_weight.shape[0], kept, got


def line_device(n_row, tokens, up_weight, hidden_grad):
    col = lax.axis_index("col").astype(jnp.int32)
    inward = [(0, 1), (3, 2)]
    outward = [(1, 0), (2, 3)]
    across = [(1, 2), (2, 1)]

    def send(x, pairs):
        return lax.ppermute(x, "col", pairs)

    rows, block = tokens.shape
    unit = rows // sum(shares)
    half = col // 2
    is_middle = ((col == 1) | (col == 2)).astype(jnp.int32)
    place = [col, col ^ 1, 2 - half, 3 * (1 - half), is_middle]
    place = jnp.stack(place + [lax.axis_index("row").astype(jnp.int32)])

    panel = gather_panel(up_weight, n_row)

    grouped = []
    at = 0
    for index, count in enumerate(groups):
        first = sum(groups[:index])
        start, at = at, at + unit * sum(shares[first : first + count])
        own = lax.slice_in_dim(tokens, start, at, axis=0)
        pair = (send(own, inward), send(own, outward))
        grouped += [(start,) + pair] * count

    early = unit * sum(shares[:ahead])
    across_own = send(lax.slice_in_dim(tokens, 0, early, axis=0), across)
    spread_own = send(across_own, outward)

    hidden = None
    input_grad = jnp.zeros((rows, block), jnp.bfloat16)
    at = 0
    for index, share in enumerate(shares):
        size = share * unit
        left = len(shares) - index
        start, out_in, mid_in = grouped[index]
        theirs = lax.slice_in_dim(out_in, at - start, at - start + size, axis=0)
        if index >= ahead:
            own = lax.slice_in_dim(tokens, at, at + size, axis=0)
            theirs = jnp.concatenate([own, theirs], axis=1)
        cross = send(theirs, across)
        spread = send(cross, outward)
        if index < ahead:
            cross = ((across_own, 0, at), (cross, 0, 0))
            spread = ((spread_own, 0, at), (spread, 0, 0))
        else:
            cross = ((cross, 0, 0), (cross, 1, 0))
            spread = ((spread, 0, 0), (spread, 1, 0))
        widths = (2, 1, 1) if left <= late_parts else (3, 1)
        hidden, *terms = chunk_call(
            place, size, tokens, out_in, mid_in, cross, spread, panel, hidden_grad, hidden, at, start, widths
        )
        if left <= late_parts:
            far, part, keep = terms
            got = send(far, inward)
            got_part = send(part, inward)
        else:
            far, keep = terms
            got = send(far, inward)
            part, got_part = far[:, 2 * block :], got[:, 2 * block :]

        def add(x, y):
            return x.astype(jnp.float32) + y.astype(jnp.float32)

        if left <= late_backs:
            far_outer = add(far[:, block : 2 * block], got[:, block : 2 * block]).astype(jnp.bfloat16)
            back_part = send(far_outer, across)
            far_middle = add(far[:, :block], got[:, :block]).astype(jnp.bfloat16)
            back_own = send(far_middle, across)
        else:
            far_sum = add(far[:, : 2 * block], got[:, : 2 * block]).astype(jnp.bfloat16)
            back = send(far_sum, across)
            back_own, back_part = back[:, :block], back[:, block:]
        partner_sum = add(part, back_part).astype(jnp.bfloat16)
        last = send(partner_sum, outward)
        total = add(keep, back_own) + got_part.astype(jnp.float32) + last.astype(jnp.float32)
        input_grad = lax.dynamic_update_slice(input_grad, total.astype(jnp.bfloat16), (at, 0))
        at += size
    return (hidden, input_grad)


def fits_line(mesh, tokens, up_weight):
    n_row, n_col = mesh.shape["row"], mesh.shape["col"]
    rows, block = tokens.shape[0] // n_row, tokens.shape[1] // n_col
    return (
        n_col == 4
        and n_row > 1
        and n_row & (n_row - 1) == 0
        and rows % (16 * sum(shares)) == 0
        and block % 128 == 0
        and up_weight.shape[1] % (128 * n_col) == 0
    )


def solution(mesh):
    specs = (P("row", "col"), P("row", "col"), P("row", "col"))

    def line_body(*blocks):
        return line_device(mesh.shape["row"], *blocks)

    def mapped(body):
        return jax.shard_map(body, mesh=mesh, in_specs=specs, out_specs=specs[:2], check_vma=False)

    ordered = mapped(line_body)

    def whole(tokens, up_weight, hidden_grad):
        if fits_line(mesh, tokens, up_weight):
            return ordered(tokens, up_weight, hidden_grad)
        return mapped(plain_device)(tokens, up_weight, hidden_grad)

    return whole
```
